32 devices in a mesh: groups: 2 (over x), expert: 16 (over z, y, core).
Axes of the slice: x: 2, y: 2, z: 4, core: 2. Of those that a mesh axis runs over, the one named last changes fastest.
Arguments:
- tokens: bfloat16 [2048, 2048], P(('groups', 'expert')), parts along dimension 0, may hold values from -6 to 6
- expert_ids: int32 [2048, 8], P(('groups', 'expert')), parts along dimension 0, may hold values from 0 to 15, as said below
- gate_weights: float32 [2048, 8], P(('groups', 'expert')), parts along dimension 0, may hold values from 0.05 to 0.5
- w_gate: bfloat16 [16, 2048, 768], P('expert'), may hold values from -0.125 to 0.125
- w_up: bfloat16 [16, 2048, 768], P('expert'), may hold values from -0.125 to 0.125
- w_down: bfloat16 [16, 768, 2048], P('expert'), may hold values from -0.21875 to 0.21875
Outputs:
- mixed: bfloat16 [2048, 2048], P(('groups', 'expert')), parts along dimension 0
The draws below stay inside these ranges and needn't reach their ends.
There are 2 independent parts, one for each index of `groups`. The reference program is written for one: setup_inputs(seed, part) draws one part's arguments, and reference() takes and returns one part's arrays. A program takes and returns all parts, laid end to end along the dimension named above; an argument that names none is the same for every part. Nothing has to cross between parts.
Inputs may be any that keep to these rules, and one draw needn't show every extreme that they name: `expert_ids`: each token names 8 different experts. Exactly 2 experts are named exactly 64 times by the tokens of every device; every other expert is named at most 28 times by the tokens of one device, and in every draw some such expert is named exactly 28 times by the tokens of every device.
All inputs are finite; a program needn't handle non-finite values.
Results may differ from the reference program's by a relative error of at most 0.0057.
Values may be sent and summed in bfloat16 or wider, within the bound.
A program may use at most 128 MiB of HBM per device.

```python
import math
from functools import partial
import jax
import jax.numpy as jnp
from jax import lax

D = 2048
FF = 768
TOP = 8
HOT = 2
TOK_DEV = 64
EXPERTS = 16
TOKENS = 1024
CAP = 64


def route_block(is_hot, base_load, extra_load, block_key):
    order_key, token_key, turn_key = jax.random.split(block_key, 3)
    shuffled = jax.random.permutation(order_key, EXPERTS).astype(jnp.int32)
    ranking = jnp.argsort(jnp.argsort(shuffled + EXPERTS * is_hot))
    expert_load = jnp.where(is_hot > 0, CAP, base_load + (ranking < extra_load).astype(jnp.int32))
    load_ends = jnp.cumsum(expert_load)
    slot_index = jnp.arange(TOK_DEV * TOP, dtype=jnp.int32)
    listing = jnp.sum((load_ends[None, :] <= slot_index[:, None]).astype(jnp.int32), axis=1)
    route_table = listing.reshape(TOP, TOK_DEV).T
    rotation = jax.random.randint(turn_key, (TOK_DEV, 1), 0, TOP)
    column = (jnp.arange(TOP, dtype=jnp.int32)[None, :] + rotation) % TOP
    route_table = jnp.take_along_axis(route_table, column, axis=1)
    return route_table[jax.random.permutation(token_key, TOK_DEV)]


def draw_expert_ids(key, part):
    hot_order = jax.random.permutation(jax.random.fold_in(key, 11), EXPERTS)
    is_hot = (hot_order < HOT).astype(jnp.int32)
    spread_rows = TOK_DEV * TOP - HOT * CAP
    base_load = spread_rows // (EXPERTS - HOT)
    extra_load = spread_rows % (EXPERTS - HOT)
    block_keys = jax.random.split(jax.random.fold_in(key, 23), TOKENS // TOK_DEV)
    routed = jax.vmap(partial(route_block, is_hot, base_load, extra_load))(block_keys)
    return routed.reshape(TOKENS, TOP).astype(jnp.int32)


def steps_of(own_key, shape, shards, least, top_value):
    loudness, own = 1.0, jax.random.fold_in(own_key, 6)
    for axis_at, parts in shards:
        steps = jnp.exp(jax.random.uniform(jax.random.fold_in(own, axis_at), (parts,), jnp.float32, least / len(shards), top_value / len(shards)))
        loudness = loudness * jnp.repeat(steps, shape[axis_at] // parts).reshape([-1 if axis == axis_at else 1 for axis in range(len(shape))])
    return loudness


def noise(rng, dims, width, most, cuts=(), kind=jnp.bfloat16):
    array = width * jax.random.normal(rng, dims, jnp.float32)
    if cuts:
        array = array * steps_of(rng, dims, cuts, -0.22, 0.18)
    return jnp.clip(array, -most, most).astype(kind)


def setup_inputs(seed: int = 0, part: int = 0) -> dict:
    key_of = jax.random.split(jax.random.key(seed), 7)
    part_keys = jax.random.split(jax.random.fold_in(key_of[6], part), 7)
    return {
        "tokens": noise(part_keys[0], (TOKENS, D), 1.0, 6.0, ((0, 16),)),
        "expert_ids": draw_expert_ids(jax.random.fold_in(jax.random.fold_in(key_of[6], part), 71), part),
        "gate_weights": jnp.clip(jnp.exp(math.log(0.5) - 2.3025851 * jax.random.uniform(part_keys[2], (TOKENS, TOP), jnp.float32) ** steps_of(part_keys[2], (TOKENS, TOP), ((0, 16),), -0.2, 0.2)), 0.05, 0.5),
        "w_gate": noise(key_of[3], (EXPERTS, D, FF), D ** -0.5, 0.125, ((0, 16),)),
        "w_up": noise(key_of[4], (EXPERTS, D, FF), D ** -0.5, 0.125, ((0, 16),)),
        "w_down": noise(key_of[5], (EXPERTS, FF, D), FF ** -0.5, 0.21875, ((0, 16),)),
    }


row_block = 128


def reference(tokens, expert_ids, gate_weights, w_gate, w_up, w_down):
    flat_ids = expert_ids.reshape(-1).astype(jnp.int32)
    slot_total = flat_ids.shape[0]
    block_count = (slot_total + row_block - 1) // row_block + EXPERTS
    total_rows = block_count * row_block
    expert_range = jnp.arange(EXPERTS, dtype=jnp.int32)
    onehot = (flat_ids[:, None] == expert_range[None, :]).astype(jnp.int32)
    per_expert = jnp.sum(onehot, axis=0)
    rank_inside = jnp.sum(jnp.cumsum(onehot, axis=0) * onehot, axis=1) - 1
    padded_count = (per_expert + row_block - 1) // row_block * row_block
    expert_start = jnp.cumsum(padded_count) - padded_count
    position = expert_start[flat_ids] + rank_inside
    token_of_slot = jnp.arange(slot_total, dtype=jnp.int32) // TOP
    source_token = jnp.full((total_rows,), -1, jnp.int32).at[position].set(token_of_slot)
    block_start = jnp.arange(block_count, dtype=jnp.int32) * row_block
    expert_end = expert_start + padded_count
    block_expert = jnp.sum((expert_end[None, :] <= block_start[:, None]).astype(jnp.int32), axis=1)
    block_expert = jnp.minimum(block_expert, EXPERTS - 1).astype(jnp.int32)

    def one_block(carry, block_pair):
        expert_now, token_slice = block_pair
        is_valid = token_slice >= 0
        picked = tokens[jnp.maximum(token_slice, 0)]
        picked = jnp.where(is_valid[:, None], picked, jnp.zeros((), tokens.dtype))
        gate_part = jnp.dot(picked, w_gate[expert_now], preferred_element_type=jnp.float32)
        up_part = jnp.dot(picked, w_up[expert_now], preferred_element_type=jnp.float32)
        hidden = (jax.nn.silu(gate_part) * up_part).astype(jnp.bfloat16)
        result = jnp.dot(hidden, w_down[expert_now], preferred_element_type=jnp.float32).astype(jnp.bfloat16)
        return carry, result

    carry_out, outputs = lax.scan(one_block, jnp.zeros((), jnp.int32), (block_expert, source_token.reshape(block_count, row_block)))
    expert_out = outputs.reshape(total_rows, D)[position].reshape(TOKENS, TOP, D)
    mixed = jnp.sum(expert_out.astype(jnp.float32) * gate_weights.astype(jnp.float32)[:, :, None], axis=1)
    return mixed.astype(jnp.bfloat16)
```

```python
import functools
import jax
import jax.numpy as jnp
from jax import lax
from jax.experimental import pallas as pl
from jax.experimental.pallas import tpu as pltpu
from jax.sharding import PartitionSpec as P

row_block = 256
pieces = 8
chunks = 4
late_chunks = 1
z_pieces = 2
hidden_tile = 256
vmem_budget = 48 * 2**20


def swiglu_rows(rows_in, weights):
    gate_part = jnp.dot(rows_in, weights[0], preferred_element_type=jnp.float32)
    up_part = jnp.dot(rows_in, weights[1], preferred_element_type=jnp.float32)
    hidden = (jax.nn.silu(gate_part) * up_part).astype(jnp.bfloat16)
    return jnp.dot(hidden, weights[2], preferred_element_type=jnp.float32).astype(jnp.bfloat16)


def run_blocks(source_rows, block_total, weights, results):

    def block_step(block_num, current):
        row_start = block_num * row_block
        rows_in = lax.dynamic_slice_in_dim(source_rows, row_start, row_block, 0)
        return lax.dynamic_update_slice_in_dim(current, swiglu_rows(rows_in, weights), row_start, 0)

    return lax.fori_loop(jnp.zeros((), jnp.int32), block_total, block_step, results)


def route_and_run(tokens, flat_ids, slot_rank, routed, capacity, device_count, own_weights):
    local_tokens, model_width = tokens.shape
    slot_total = flat_ids.shape[0]
    top_count = slot_total // local_tokens
    buffer_rows = device_count * capacity
    padded_rows = (buffer_rows + row_block - 1) // row_block * row_block
    send_slot = jnp.where(routed, flat_ids * capacity + slot_rank, buffer_rows)
    token_of_slot = jnp.arange(slot_total, dtype=jnp.int32) // top_count
    source_row = jnp.zeros((buffer_rows,), jnp.int32).at[send_slot].set(token_of_slot, mode="drop")
    slot_filled = jnp.zeros((buffer_rows,), jnp.int32).at[send_slot].set(1, mode="drop")
    send_counts = jnp.sum(slot_filled.reshape(device_count, capacity), axis=1)
    outgoing = jnp.where(slot_filled[:, None] > 0, tokens[source_row], jnp.zeros((), jnp.bfloat16))
    outgoing = outgoing.reshape(device_count, capacity, model_width)
    count_column = send_counts.astype(jnp.bfloat16).reshape(device_count, 1)
    incoming, arrived = (
        lax.all_to_all(outgoing, "expert", split_axis=0, concat_axis=0, tiled=True),
        lax.all_to_all(count_column, "expert", split_axis=0, concat_axis=0, tiled=True),
    )
    arrived_counts = arrived.reshape(-1).astype(jnp.int32)
    offsets = jnp.cumsum(arrived_counts) - arrived_counts
    live_total = jnp.sum(arrived_counts)
    slot_index = jnp.arange(buffer_rows, dtype=jnp.int32)
    source_of = slot_index // capacity
    within = slot_index % capacity
    is_live = within < arrived_counts[source_of]
    packed_pos = offsets[source_of] + within
    target_pos = jnp.where(is_live, packed_pos, padded_rows)
    compact_source = (
        jnp.full((padded_rows,), buffer_rows, jnp.int32).at[target_pos].set(slot_index, mode="drop")
    )
    flat_incoming = jnp.concatenate(
        [incoming.reshape(buffer_rows, model_width), jnp.zeros((1, model_width), jnp.bfloat16)],
        axis=0,
    )
    compact = flat_incoming[compact_source]
    block_need = (live_total + row_block - 1) // row_block
    results = run_blocks(
        compact, block_need, own_weights, jnp.zeros((padded_rows, model_width), jnp.bfloat16)
    )
    back_slots = results[jnp.where(is_live, packed_pos, 0)]
    back_slots = jnp.where(is_live[:, None], back_slots, jnp.zeros((), jnp.bfloat16))
    back_slots = back_slots.reshape(device_count, capacity, model_width)
    returned_rows = lax.all_to_all(back_slots, "expert", split_axis=0, concat_axis=0, tiled=True)
    picked = returned_rows.reshape(buffer_rows, model_width)[jnp.where(routed, send_slot, 0)]
    return jnp.where(routed[:, None], picked, jnp.zeros((), jnp.bfloat16))


def visit_order(depth, place):
    return sorted(range(depth), key=lambda g: (abs(g - place), g if 2 * place < depth else -g))


def fused_kernel(
    depth, x_hbm, ids_ref, gates_ref, wg_hbm, wu_hbm, wd_hbm, out_ref,
    rows, tiles, wg, wu, wd, hid, part, a_in, y_out, y_in, c_out, c_in,
    w_sem, own_sem, sx, rx, st, rt, sa, ra, sy, ry, sc, rc,
):
    f32, bf16 = jnp.float32, jnp.bfloat16
    local, width = x_hbm.shape
    inner = wg.shape[1]
    span = width // pieces
    me = lax.axis_index("expert")
    c = lax.rem(me, 2)
    y = lax.rem(me // 2, 2)
    z = me // 4
    own_slot = y * 2 + c
    far_slot = (1 - y) * 2 + c
    group_of = []
    for step in range(depth):
        g = jnp.int32(0)
        for place in range(depth):
            g = g + jnp.where(z == place, visit_order(depth, place)[step], 0)
        group_of.append(g)
    sibling = {"expert": (z * 2 + y) * 2 + (1 - c)}
    across = {"expert": (z * 2 + (1 - y)) * 2 + c}

    def along(place):
        return {"expert": (place * 2 + y) * 2 + c}

    has_up, has_down = z < depth - 1, z > 0
    corner = (z == 0) | (z == depth - 1)

    own_copies = [pltpu.make_async_copy(x_hbm, rows.at[z, own_slot], own_sem.at[0])]
    weight_copies = [
        pltpu.make_async_copy(wg_hbm.at[0], wg, w_sem.at[0]),
        pltpu.make_async_copy(wu_hbm.at[0], wu, w_sem.at[1]),
        pltpu.make_async_copy(wd_hbm.at[0], wd, w_sem.at[2]),
    ]

    def signal(target):
        pl.semaphore_signal(barrier, inc=1, device_id=target, device_id_type=pl.DeviceIdType.MESH)

    barrier = pltpu.get_barrier_semaphore()
    signal(sibling)
    signal(across)
    pl.when(has_up)(lambda: signal(along(z + 1)))
    pl.when(has_down)(lambda: signal(along(z - 1)))

    expert_row = lax.broadcasted_iota(jnp.int32, (tiles.shape[2], local), 0)
    dense = jnp.zeros((tiles.shape[2], local), f32)
    for k in range(ids_ref.shape[0]):
        dense += jnp.where(ids_ref[k : k + 1, :] == expert_row, gates_ref[k : k + 1, :], 0.0)
    tiles[z, own_slot] = jnp.zeros(tiles.shape[2:], f32)
    tiles[z, own_slot, :, :local] = dense

    pl.semaphore_wait(barrier, 2 + has_up.astype(jnp.int32) + has_down.astype(jnp.int32))

    def remote(src, dst, send, recv, target):
        return pltpu.make_async_remote_copy(
            src_ref=src, dst_ref=dst, send_sem=send, recv_sem=recv,
            device_id=target, device_id_type=pl.DeviceIdType.MESH,
        )

    pending = []
    counts = {"x": 0, "t": 0}

    def launch(copies, cond=None):
        def go():
            for copy in copies:
                copy.start()
        if cond is None:
            go()
        else:
            pl.when(cond)(go)
        pending.append((copies, cond))

    chunk_rows = local // chunks
    early = list(range(chunks - late_chunks))
    late = list(range(chunks - late_chunks, chunks))

    def chunk_copy(g, slot, h, src, send, target):
        part_rows = pl.ds(h * chunk_rows, chunk_rows)
        return remote(src.at[part_rows], rows.at[g, slot, part_rows], send, rx.at[g, slot, h], target)

    def tile_copy(g, slot, send, target):
        return remote(tiles.at[g, slot], tiles.at[g, slot], send, rt.at[g, slot], target)

    def push(g, slot, h, target, cond=None, src=None):
        src = rows.at[g, slot] if src is None else src
        copies = [chunk_copy(g, slot, h, src, sx.at[counts["x"]], target)]
        counts["x"] += 1
        launch(copies, cond)

    def push_tile(g, slot, target, cond=None):
        copies = [tile_copy(g, slot, st.at[counts["t"]], target)]
        counts["t"] += 1
        launch(copies, cond)

    def arrive(g, slot, h):
        chunk_copy(g, slot, h, rows.at[g, slot], sx.at[0], sibling).wait_recv()
        if h == 0:
            tile_copy(g, slot, st.at[0], sibling).wait_recv()

    for h in range(chunks):
        push(z, own_slot, h, along(z + 1), has_up, src=x_hbm)
        push(z, own_slot, h, along(z - 1), has_down, src=x_hbm)
        push(z, own_slot, (late + early)[h], across, src=x_hbm)
        if h == 0:
            push_tile(z, own_slot, along(z + 1), has_up)
            push_tile(z, own_slot, along(z - 1), has_down)
            push_tile(z, own_slot, across)
    for h in range(chunks):
        push(z, own_slot, h, sibling, src=x_hbm)
    push_tile(z, own_slot, sibling)
    for copy in own_copies + weight_copies:
        copy.start()

    @pl.when(z == 0)
    def _():
        c_in[0] = jnp.zeros(c_in.shape[1:], bf16)

    @pl.when(z == depth - 1)
    def _():
        c_in[1] = jnp.zeros(c_in.shape[1:], bf16)

    def onward_of(g):
        onward = jnp.where(g < z, z + 1, z - 1)
        return along(onward), (onward >= 0) & (onward < depth)

    def relay_z(step, h):
        g = group_of[step]
        arrive(g, own_slot, h)
        target, cond = onward_of(g)
        push(g, own_slot, h, target, cond)
        if h in early:
            push(g, own_slot, h, across)
        if h == 0:
            push_tile(g, own_slot, target, cond)
            push_tile(g, own_slot, across)
        push(g, own_slot, h, sibling)
        if h == 0:
            push_tile(g, own_slot, sibling)

    def relay_far_z(step):
        g = group_of[step]
        for h in late:
            arrive(g, far_slot, h)
            target, cond = onward_of(g)
            push(g, far_slot, h, target, cond)
            push(g, far_slot, h, sibling)

    def relay_y(step, h):
        g = group_of[step]
        arrive(g, far_slot, h)
        if step == 0 and h in late:
            push(g, far_slot, h, along(z + 1), has_up)
            push(g, far_slot, h, along(z - 1), has_down)
        push(g, far_slot, h, sibling)
        if h == 0:
            push_tile(g, far_slot, sibling)

    def await_sibling(step, k):
        g = group_of[step]
        column = y if k == 0 else 1 - y
        for h in range(chunks):
            arrive(g, column * 2 + 1 - c, h)
        if step == 0 and k == 0:
            for copy in own_copies + weight_copies:
                copy.wait()

    def column_of(k):
        return y if k == 0 else 1 - y

    def run_hidden(step, k):
        await_sibling(step, k)
        g = group_of[step]
        for j in range(inner // hidden_tile):
            cols = pl.ds(j * hidden_tile, hidden_tile)
            block = rows[g, pl.ds(column_of(k) * 2, 2)].reshape(2 * local, width)
            gate = jnp.dot(block, wg[:, cols], preferred_element_type=f32)
            up = jnp.dot(block, wu[:, cols], preferred_element_type=f32)
            hid[:, cols] = (gate / (1.0 + jnp.exp(-gate)) * up).astype(bf16)

    ranges = [(0, z_pieces), (z_pieces, (pieces + z_pieces) // 2), ((pieces + z_pieces) // 2, pieces)]

    def pair_copy(step, k, r):
        lo, hi = ranges[r]
        some = pl.ds(lo, hi - lo)
        return remote(
            part.at[step, k, 1 - c, some], a_in.at[step, k, some],
            sa.at[step, k, r], ra.at[step, k, r], sibling,
        )

    def run_out(step, k):
        g = group_of[step]
        lanes = tiles.shape[3]
        lane = lax.broadcasted_iota(jnp.int32, (local, lanes), 1)
        line = lax.broadcasted_iota(jnp.int32, (local, lanes), 0)
        own_row = lax.broadcasted_iota(jnp.int32, tiles.shape[2:], 0) == me
        scales = []
        for core in range(2):
            mine = jnp.sum(
                jnp.where(own_row, tiles[g, column_of(k) * 2 + core], 0.0), axis=0, keepdims=True
            )
            spread = jnp.broadcast_to(mine, (local, lanes))
            scales.append(jnp.sum(jnp.where(lane == line, spread, 0.0), axis=1, keepdims=True))
        for r, (lo, hi) in enumerate(ranges):
            for p in range(lo, hi):
                result = jnp.dot(hid[...], wd[:, pl.ds(p * span, span)], preferred_element_type=f32)
                for core in range(2):
                    scaled = result[core * local : (core + 1) * local] * scales[core]
                    part[step, k, core, p] = scaled.astype(bf16)
            launch([pair_copy(step, k, r)])

    paired = set()

    def pair_sum(step, k, p):
        r = [lo <= p < hi for lo, hi in ranges].index(True)
        if (step, k, r) not in paired:
            paired.add((step, k, r))
            pair_copy(step, k, r).wait_recv()
        return part[step, k, c, p].astype(f32) + a_in[step, k, p].astype(f32)

    def await_pairs(step, k, lo, hi):
        for r, (first, last) in enumerate(ranges):
            if first < hi and last > lo and (step, k, r) not in paired:
                paired.add((step, k, r))
                pair_copy(step, k, r).wait_recv()

    def across_copy(step, p):
        return remote(
            y_out.at[step, p], y_in.at[step, p], sy.at[step, p], ry.at[step, p], across
        )

    def send_across(step):
        for p in range(z_pieces, pieces):
            y_out[step, p] = pair_sum(step, 1, p).astype(bf16)
            launch([across_copy(step, p)])

    def chain_copy(step, way, g, j, target):
        return remote(
            c_out.at[step, j], c_in.at[way, g, j], sc.at[step, j], rc.at[way, g, j], target
        )

    def hop(step, j, value, cond=None, first=False):
        g = group_of[step]
        way = jnp.where(g > z, 0, 1)
        copy = chain_copy(step, way, g, j, along(jnp.where(g > z, z + 1, z - 1)))

        def go():
            if first:
                c_out[step, j] = value().astype(bf16)
            else:
                pl.when(jnp.logical_not(corner))(
                    lambda: chain_copy(0, way, g, j, sibling).wait_recv()
                )
                c_out[step, j] = (value() + c_in[way, g, j].astype(f32)).astype(bf16)
            copy.start()

        if cond is None:
            go()
        else:
            pl.when(cond)(go)

    def note_hop(step, j):
        g = group_of[step]
        way = jnp.where(g > z, 0, 1)
        pending.append(
            ([chain_copy(step, way, g, j, along(jnp.where(g > z, z + 1, z - 1)))], None)
        )

    def chain_split(step, k, cond=None, first=False):
        await_pairs(step, k, 0, z_pieces)
        for q in range(z_pieces):
            j = q if k == 0 else pieces + q
            hop(step, j, lambda: pair_sum(step, k, q), cond, first)

    def chain_whole(step):
        for p in range(z_pieces, pieces):
            across_copy(step, p).wait_recv()
            hop(step, p, lambda: pair_sum(step, 0, p) + y_in[step, p].astype(f32))

    def await_ends(j):
        pl.when(has_down)(lambda: chain_copy(0, 0, z, j, sibling).wait_recv())
        pl.when(has_up)(lambda: chain_copy(0, 1, z, j, sibling).wait_recv())

    def ends(j):
        return c_in[0, z, j].astype(f32) + c_in[1, z, j].astype(f32)

    def early_chain(step):
        if 0 < step < depth:
            for k in range(2):
                chain_split(step, k, corner, True)

    last = depth - 1
    for h in late:
        relay_y(0, h)
    for t in range(1, depth):
        for h in range(chunks):
            relay_z(t, h)
            if h in early:
                relay_y(t - 1, h)
            if h == 0:
                run_hidden(t - 1, 0)
            if h == 1:
                run_out(t - 1, 0)
                if t > 1:
                    relay_far_z(t)
            if h == 2:
                if t >= 2:
                    early_chain(t - 2)
        if t == 1:
            relay_far_z(t)
        run_hidden(t - 1, 1)
        run_out(t - 1, 1)
    relay_y(last, 0)
    run_hidden(last, 0)
    early_chain(last - 1)
    for h in early[1:]:
        relay_y(last, h)
    run_out(last, 0)
    if depth > 2:
        send_across(last - 1)
    run_hidden(last, 1)
    run_out(last, 1)
    middle = jnp.logical_not(corner)
    order = ([last - 1] if depth > 2 else []) + [last] + list(range(last - 2, 0, -1))
    sends = order[1 if depth > 2 else 0 :] + [0]
    for at, step in enumerate(order):
        if at < len(sends):
            send_across(sends[at])
        for k in range(2):
            if step == last:
                chain_split(step, k)
            else:
                chain_split(step, k, middle)
        chain_whole(step)
    for step in sends[len(order) :]:
        send_across(step)
    for q in range(z_pieces):
        await_ends(pieces + q)
        y_out[0, q] = (pair_sum(0, 1, q) + ends(pieces + q)).astype(bf16)
        launch([across_copy(0, q)])
    for p in list(range(z_pieces, pieces)) + list(range(z_pieces)):
        await_ends(p)
        total = pair_sum(0, 0, p) + ends(p)
        across_copy(0, p).wait_recv()
        out_ref[:, pl.ds(p * span, span)] = (total + y_in[0, p].astype(f32)).astype(bf16)
    for step in range(1, depth):
        for j in range(pieces + z_pieces):
            note_hop(step, j)
    for copies, cond in pending:
        def finish(copies=copies):
            for copy in copies:
                copy.wait_send()
        if cond is None:
            finish()
        else:
            pl.when(cond)(finish)


def fused_layer(tokens, ids, gates, w_gate, w_up, w_down, expert_total, depth):
    local, width = tokens.shape
    inner = w_gate.shape[2]
    bf16, f32 = jnp.bfloat16, jnp.float32
    dma = pltpu.SemaphoreType.DMA
    anywhere = pl.BlockSpec(memory_space=pl.ANY)
    inside = pl.BlockSpec(memory_space=pltpu.VMEM)
    span = width // pieces
    sends = depth * (6 * chunks + 2)
    lots = pieces + z_pieces
    return pl.pallas_call(
        functools.partial(fused_kernel, depth),
        out_shape=jax.ShapeDtypeStruct((local, width), bf16),
        in_specs=[anywhere, inside, inside] + [anywhere] * 3,
        out_specs=pl.BlockSpec(memory_space=pltpu.VMEM),
        scratch_shapes=[
            pltpu.VMEM((depth, 4, local, width), bf16),
            pltpu.VMEM((depth, 4, expert_total, 128), f32),
            pltpu.VMEM((width, inner), bf16),
            pltpu.VMEM((width, inner), bf16),
            pltpu.VMEM((inner, width), bf16),
            pltpu.VMEM((2 * local, inner), bf16),
            pltpu.VMEM((depth, 2, 2, pieces, local, span), bf16),
            pltpu.VMEM((depth, 2, pieces, local, span), bf16),
            pltpu.VMEM((depth, pieces, local, span), bf16),
            pltpu.VMEM((depth, pieces, local, span), bf16),
            pltpu.VMEM((depth, lots, local, span), bf16),
            pltpu.VMEM((2, depth, lots, local, span), bf16),
            dma((3,)), dma((1,)),
            dma((sends,)), dma((depth, 4, chunks)), dma((5 * depth,)), dma((depth, 4)),
            dma((depth, 2, 3)), dma((depth, 2, 3)),
            dma((depth, pieces)), dma((depth, pieces)),
            dma((depth, lots)), dma((2, depth, lots)),
        ],
        compiler_params=pltpu.CompilerParams(
            collective_id=0, has_side_effects=True, vmem_limit_bytes=60 * 2**20
        ),
    )(tokens, ids, gates, w_gate, w_up, w_down)


def fits_fused(device_count, local_tokens, model_width, inner):
    gathered = 2 * device_count * local_tokens * model_width
    weights = 6 * model_width * inner
    return (
        device_count % 4 == 0
        and device_count >= 8
        and local_tokens in (64, 128)
        and local_tokens % (16 * chunks) == 0
        and model_width % (pieces * 128) == 0
        and inner % hidden_tile == 0
        and 4 * gathered + weights <= vmem_budget
    )


def shards(tokens, expert_ids, gate_weights, w_gate, w_up, w_down):
    device_count = lax.axis_size("expert")
    local_tokens, model_width = tokens.shape
    top_count = expert_ids.shape[1]
    expert_total = device_count * w_gate.shape[0]
    capacity = min(
        local_tokens, 4 * ((local_tokens * top_count + expert_total - 1) // expert_total)
    )
    if fits_fused(device_count, local_tokens, model_width, w_gate.shape[2]):
        return fused_layer(
            tokens, expert_ids.T, gate_weights.T, w_gate, w_up, w_down, expert_total, device_count // 4
        )
    flat_ids = expert_ids.reshape(-1)
    slot_total = flat_ids.shape[0]
    expert_range = jnp.arange(device_count, dtype=jnp.int32)
    onehot = (flat_ids[:, None] == expert_range[None, :]).astype(jnp.int32)
    slot_rank = jnp.sum(jnp.cumsum(onehot, axis=0) * onehot, axis=1) - 1
    own_weights = (w_gate[0], w_up[0], w_down[0])
    routed = jnp.ones((slot_total,), jnp.bool_)
    slot_values = route_and_run(
        tokens, flat_ids, slot_rank, routed, capacity, device_count, own_weights
    )
    picked = slot_values.reshape(local_tokens, top_count, model_width)
    mixed = jnp.sum(picked.astype(jnp.float32) * gate_weights[:, :, None], axis=1)
    return mixed.astype(jnp.bfloat16)


def solution(mesh):
    placed = (
        P(("groups", "expert"), None),
        P(("groups", "expert"), None),
        P(("groups", "expert"), None),
        P("expert", None, None),
        P("expert", None, None),
        P("expert", None, None),
    )
    return jax.shard_map(
        shards, mesh=mesh, in_specs=placed, out_specs=P(("groups", "expert"), None), check_vma=False
    )
```

```python
import functools
import jax
import jax.numpy as jnp
from jax import lax
from jax.experimental import pallas as pl
from jax.experimental.pallas import tpu as pltpu
from jax.sharding import PartitionSpec as P

row_block = 256
pieces = 4
chunks = 4
late_chunks = 1
z_pieces = 0
hidden_tile = 256
vmem_budget = 48 * 2**20


def swiglu_rows(rows_in, weights):
    gate_part = jnp.dot(rows_in, weights[0], preferred_element_type=jnp.float32)
    up_part = jnp.dot(rows_in, weights[1], preferred_element_type=jnp.float32)
    hidden = (jax.nn.silu(gate_part) * up_part).astype(jnp.bfloat16)
    return jnp.dot(hidden, weights[2], preferred_element_type=jnp.float32).astype(jnp.bfloat16)


def run_blocks(source_rows, block_total, weights, results):

    def block_step(block_num, current):
        row_start = block_num * row_block
        rows_in = lax.dynamic_slice_in_dim(source_rows, row_start, row_block, 0)
        return lax.dynamic_update_slice_in_dim(current, swiglu_rows(rows_in, weights), row_start, 0)

    return lax.fori_loop(jnp.zeros((), jnp.int32), block_total, block_step, results)


def route_and_run(tokens, flat_ids, slot_rank, routed, capacity, device_count, own_weights):
    local_tokens, model_width = tokens.shape
    slot_total = flat_ids.shape[0]
    top_count = slot_total // local_tokens
    buffer_rows = device_count * capacity
    padded_rows = (buffer_rows + row_block - 1) // row_block * row_block
    send_slot = jnp.where(routed, flat_ids * capacity + slot_rank, buffer_rows)
    token_of_slot = jnp.arange(slot_total, dtype=jnp.int32) // top_count
    source_row = jnp.zeros((buffer_rows,), jnp.int32).at[send_slot].set(token_of_slot, mode="drop")
    slot_filled = jnp.zeros((buffer_rows,), jnp.int32).at[send_slot].set(1, mode="drop")
    send_counts = jnp.sum(slot_filled.reshape(device_count, capacity), axis=1)
    outgoing = jnp.where(slot_filled[:, None] > 0, tokens[source_row], jnp.zeros((), jnp.bfloat16))
    outgoing = outgoing.reshape(device_count, capacity, model_width)
    count_column = send_counts.astype(jnp.bfloat16).reshape(device_count, 1)
    incoming, arrived = (
        lax.all_to_all(outgoing, "expert", split_axis=0, concat_axis=0, tiled=True),
        lax.all_to_all(count_column, "expert", split_axis=0, concat_axis=0, tiled=True),
    )
    arrived_counts = arrived.reshape(-1).astype(jnp.int32)
    offsets = jnp.cumsum(arrived_counts) - arrived_counts
    live_total = jnp.sum(arrived_counts)
    slot_index = jnp.arange(buffer_rows, dtype=jnp.int32)
    source_of = slot_index // capacity
    within = slot_index % capacity
    is_live = within < arrived_counts[source_of]
    packed_pos = offsets[source_of] + within
    target_pos = jnp.where(is_live, packed_pos, padded_rows)
    compact_source = (
        jnp.full((padded_rows,), buffer_rows, jnp.int32).at[target_pos].set(slot_index, mode="drop")
    )
    flat_incoming = jnp.concatenate(
        [incoming.reshape(buffer_rows, model_width), jnp.zeros((1, model_width), jnp.bfloat16)],
        axis=0,
    )
    compact = flat_incoming[compact_source]
    block_need = (live_total + row_block - 1) // row_block
    results = run_blocks(
        compact, block_need, own_weights, jnp.zeros((padded_rows, model_width), jnp.bfloat16)
    )
    back_slots = results[jnp.where(is_live, packed_pos, 0)]
    back_slots = jnp.where(is_live[:, None], back_slots, jnp.zeros((), jnp.bfloat16))
    back_slots = back_slots.reshape(device_count, capacity, model_width)
    returned_rows = lax.all_to_all(back_slots, "expert", split_axis=0, concat_axis=0, tiled=True)
    picked = returned_rows.reshape(buffer_rows, model_width)[jnp.where(routed, send_slot, 0)]
    return jnp.where(routed[:, None], picked, jnp.zeros((), jnp.bfloat16))


def visit_order(depth, place):
    return sorted(range(depth), key=lambda g: (abs(g - place), g if 2 * place < depth else -g))


def fused_kernel(
    depth, x_hbm, ids_ref, gates_ref, wg_hbm, wu_hbm, wd_hbm, out_ref,
    rows, tiles, wg, wu, wd, hid, part, a_in, y_out, y_in, c_out, c_in,
    w_sem, own_sem, sx, rx, st, rt, sa, ra, sy, ry, sc, rc,
):
    f32, bf16 = jnp.float32, jnp.bfloat16
    local, width = x_hbm.shape
    inner = wg.shape[1]
    span = width // pieces
    me = lax.axis_index("expert")
    c = lax.rem(me, 2)
    y = lax.rem(me // 2, 2)
    z = me // 4
    own_slot = y * 2 + c
    far_slot = (1 - y) * 2 + c
    group_of = []
    for step in range(depth):
        g = jnp.int32(0)
        for place in range(depth):
            g = g + jnp.where(z == place, visit_order(depth, place)[step], 0)
        group_of.append(g)
    sibling = {"expert": (z * 2 + y) * 2 + (1 - c)}
    across = {"expert": (z * 2 + (1 - y)) * 2 + c}

    def along(place):
        return {"expert": (place * 2 + y) * 2 + c}

    has_up, has_down = z < depth - 1, z > 0
    corner = (z == 0) | (z == depth - 1)

    own_copies = [pltpu.make_async_copy(x_hbm, rows.at[z, own_slot], own_sem.at[0])]
    weight_copies = [
        pltpu.make_async_copy(wg_hbm.at[0], wg, w_sem.at[0]),
        pltpu.make_async_copy(wu_hbm.at[0], wu, w_sem.at[1]),
        pltpu.make_async_copy(wd_hbm.at[0], wd, w_sem.at[2]),
    ]

    def signal(target):
        pl.semaphore_signal(barrier, inc=1, device_id=target, device_id_type=pl.DeviceIdType.MESH)

    barrier = pltpu.get_barrier_semaphore()
    signal(sibling)
    signal(across)
    pl.when(has_up)(lambda: signal(along(z + 1)))
    pl.when(has_down)(lambda: signal(along(z - 1)))

    expert_row = lax.broadcasted_iota(jnp.int32, (tiles.shape[3], local), 0)
    dense = jnp.zeros((tiles.shape[3], local), f32)
    for k in range(ids_ref.shape[0]):
        dense += jnp.where(ids_ref[k : k + 1, :] == expert_row, gates_ref[k : k + 1, :], 0.0)
    tiles[z, c, y] = jnp.zeros(tiles.shape[3:], f32)
    tiles[z, c, y, :, :local] = dense

    pl.semaphore_wait(barrier, 2 + has_up.astype(jnp.int32) + has_down.astype(jnp.int32))

    def remote(src, dst, send, recv, target):
        return pltpu.make_async_remote_copy(
            src_ref=src, dst_ref=dst, send_sem=send, recv_sem=recv,
            device_id=target, device_id_type=pl.DeviceIdType.MESH,
        )

    chunk_rows = local // chunks
    early = list(range(chunks - late_chunks))
    late = list(range(chunks - late_chunks, chunks))
    split = len(early) * chunk_rows
    both = [(0, split), (split, local)]
    places = {}

    def place(name):
        return sx.at[places.setdefault(name, len(places))]

    def block(g, slot, lo, hi, name, recv, target, src=None):
        some = pl.ds(lo, hi - lo)
        source = rows.at[g, slot] if src is None else src
        return remote(source.at[some], rows.at[g, slot, some], place(name), recv, target)

    def chunk(g, slot, h, name, target, src=None, recv=None):
        recv = rx.at[g, slot, h] if recv is None else recv
        return block(g, slot, h * chunk_rows, (h + 1) * chunk_rows, name, recv, target, src)

    def across_chunk(g, slot, h, name, src=None):
        return chunk(g, slot, h, name, across, src, rx.at[g, slot, 0 if h in early else h])

    def whole(g, slot, name, target, src=None):
        return block(g, slot, 0, local, name, rx.at[g, slot, 0], target, src)

    def tile_column():
        return remote(tiles.at[z, c], tiles.at[z, c], st.at[1], rt.at[0], sibling)

    def tile_layer(g, send, target):
        return remote(tiles.at[g], tiles.at[g], st.at[send], rt.at[2 + g], target)

    own_tile = remote(tiles.at[z, c, y], tiles.at[z, c, y], st.at[0], rt.at[1], across)
    own_tile.start()
    for h in range(chunks):
        pl.when(has_up)(lambda: chunk(z, own_slot, h, "up", along(z + 1), x_hbm).start())
        pl.when(has_down)(lambda: chunk(z, own_slot, h, "down", along(z - 1), x_hbm).start())
        across_chunk(z, own_slot, (late + early)[h], "across", x_hbm).start()
    whole(z, own_slot, "sibling", sibling, x_hbm).start()
    for copy in own_copies + weight_copies:
        copy.start()

    @pl.when(z == 0)
    def _():
        c_in[0, 0] = jnp.zeros(c_in.shape[2:], bf16)

    @pl.when(z == depth - 1)
    def _():
        c_in[1, z] = jnp.zeros(c_in.shape[2:], bf16)

    def share_tiles():
        own_tile.wait_recv()
        tile_column().start()
        tile_column().wait_recv()
        pl.when(has_up)(lambda: tile_layer(z, 2, along(z + 1)).start())
        pl.when(has_down)(lambda: tile_layer(z, 3, along(z - 1)).start())

    def ways_of(d):
        return [
            (0, z + d, z + d < depth, along(z - 1), has_down),
            (1, z - d, z - d >= 0, along(z + 1), has_up),
        ]

    def relay_z(d, h):
        for way, g, exists, onward, more in ways_of(d):
            @pl.when(exists)
            def _(way=way, g=g, onward=onward, more=more):
                chunk(g, own_slot, h, "sibling", sibling).wait_recv()
                pl.when(more)(lambda: chunk(g, own_slot, h, (d, way, 0), onward).start())
                if h in early:
                    across_chunk(g, own_slot, h, (d, way, 1)).start()
                if h == chunks - 1:
                    whole(g, own_slot, (d, way, 2), sibling).start()
                    tile_layer(g, 0, sibling).wait_recv()
                    pl.when(more)(lambda: tile_layer(g, 2 + 2 * d + way, onward).start())

    def relay_far_z(d):
        for way, g, exists, onward, more in ways_of(d):
            @pl.when(exists)
            def _(way=way, g=g, onward=onward, more=more):
                for h in late:
                    chunk(g, far_slot, h, "sibling", sibling).wait_recv()
                    pl.when(more)(lambda: chunk(g, far_slot, h, (d, way, 3), onward).start())

    def relay_far_y(d):
        for way, g, exists, _, _ in ways_of(d):
            @pl.when(exists)
            def _(way=way, g=g):
                block(g, far_slot, 0, split, "sibling", rx.at[g, far_slot, 0], sibling).wait_recv()
                whole(g, far_slot, (d, way, 4), sibling).start()

    def relay_late():
        for h in late:
            chunk(z, far_slot, h, "sibling", sibling).wait_recv()
            pl.when(has_up)(lambda: chunk(z, far_slot, h, "far_up", along(z + 1)).start())
            pl.when(has_down)(lambda: chunk(z, far_slot, h, "far_down", along(z - 1)).start())

    def relay_own_y():
        block(z, far_slot, 0, split, "sibling", rx.at[z, far_slot, 0], sibling).wait_recv()
        whole(z, far_slot, "far_sibling", sibling).start()

    def sent(g, slot, lo, hi, name):
        if hi > lo:
            block(g, slot, lo, hi, name, rx.at[g, slot, 0], sibling).wait_send()

    def finish_gather():
        own_tile.wait_send()
        tile_column().wait_send()
        sent(z, own_slot, 0, local, "across")
        sent(z, own_slot, 0, local, "sibling")
        sent(z, far_slot, 0, local, "far_sibling")

        @pl.when(has_up)
        def _():
            sent(z, own_slot, 0, local, "up")
            sent(z, far_slot, split, local, "far_up")
            tile_layer(z, 2, sibling).wait_send()

        @pl.when(has_down)
        def _():
            sent(z, own_slot, 0, local, "down")
            sent(z, far_slot, split, local, "far_down")
            tile_layer(z, 3, sibling).wait_send()

        for d in range(1, depth):
            for way, g, exists, _, more in ways_of(d):
                @pl.when(exists)
                def _(way=way, g=g, more=more):
                    sent(g, own_slot, 0, split, (d, way, 1))
                    sent(g, own_slot, 0, local, (d, way, 2))
                    sent(g, far_slot, 0, local, (d, way, 4))

                    @pl.when(more)
                    def _():
                        sent(g, own_slot, 0, local, (d, way, 0))
                        sent(g, far_slot, split, local, (d, way, 3))
                        tile_layer(g, 2 + 2 * d + way, sibling).wait_send()

    def await_sibling(step, k):
        g = group_of[step]
        whole(g, column_of(k) * 2 + 1 - c, "sibling", sibling).wait_recv()
        if step == 0 and k == 0:
            for copy in own_copies + weight_copies:
                copy.wait()

    def column_of(k):
        return y if k == 0 else 1 - y

    def run_hidden(step, k, j):
        if j == 0:
            await_sibling(step, k)
        g = group_of[step]
        cols = pl.ds(j * hidden_tile, hidden_tile)
        lines = rows[g, pl.ds(column_of(k) * 2, 2)].reshape(2 * local, width)
        gate = jnp.dot(lines, wg[:, cols], preferred_element_type=f32)
        up = jnp.dot(lines, wu[:, cols], preferred_element_type=f32)
        hid[:, cols] = (gate / (1.0 + jnp.exp(-gate)) * up).astype(bf16)

    def units(step, k):
        tiles_of = [
            functools.partial(run_hidden, step, k, j) for j in range(inner // hidden_tile)
        ]
        return tiles_of + [functools.partial(run_out, step, k)]

    ranges = [(0, pieces // 2), (pieces // 2, pieces)]

    def pair_copy(step, k, r):
        lo, hi = ranges[r]
        some = pl.ds(lo, hi - lo)
        return remote(
            part.at[step, k, 1 - c, some], a_in.at[step, k, some],
            sa.at[step, k], ra.at[step, k, r], sibling,
        )

    def run_out(step, k):
        g = group_of[step]
        lanes = tiles.shape[4]
        lane = lax.broadcasted_iota(jnp.int32, (local, lanes), 1)
        line = lax.broadcasted_iota(jnp.int32, (local, lanes), 0)
        own_row = lax.broadcasted_iota(jnp.int32, tiles.shape[3:], 0) == me
        scales = []
        for core in range(2):
            mine = jnp.sum(
                jnp.where(own_row, tiles[g, core, column_of(k)], 0.0), axis=0, keepdims=True
            )
            spread = jnp.broadcast_to(mine, (local, lanes))
            scales.append(jnp.sum(jnp.where(lane == line, spread, 0.0), axis=1, keepdims=True))
        for r, (lo, hi) in enumerate(ranges):
            for p in range(lo, hi):
                result = jnp.dot(hid[...], wd[:, pl.ds(p * span, span)], preferred_element_type=f32)
                for core in range(2):
                    scaled = result[core * local : (core + 1) * local] * scales[core]
                    part[step, k, core, p] = scaled.astype(bf16)
            pair_copy(step, k, r).start()

    paired = set()

    def pair_sum(step, k, p):
        r = [lo <= p < hi for lo, hi in ranges].index(True)
        if (step, k, r) not in paired:
            paired.add((step, k, r))
            pair_copy(step, k, r).wait_recv()
        return part[step, k, c, p].astype(f32) + a_in[step, k, p].astype(f32)

    def await_pairs(step, k, lo, hi):
        for r, (first, last) in enumerate(ranges):
            if first < hi and last > lo and (step, k, r) not in paired:
                paired.add((step, k, r))
                pair_copy(step, k, r).wait_recv()

    def across_copy(step, p):
        return remote(
            y_out.at[step, p], y_in.at[step, p], sy.at[step], ry.at[step, p], across
        )

    def send_across(step):
        for p in range(z_pieces, pieces):
            y_out[step, p] = pair_sum(step, 1, p).astype(bf16)
            across_copy(step, p).start()

    def chain_copy(step, way, g, j, target):
        return remote(
            c_out.at[step, j], c_in.at[way, g, j], sc.at[step], rc.at[way, g, j], target
        )

    last = depth - 1
    middle = jnp.logical_not(corner)

    def hop(step, j, value, relay):
        g = group_of[step]
        way = jnp.where(g > z, 0, 1)
        place_to = jnp.where(g > z, z + 1, z - 1)
        if relay:
            chain_copy(0, way, g, j, sibling).wait_recv()
            value = value + c_in[way, g, j].astype(f32)
        c_out[step, j] = value.astype(bf16)
        chain_copy(step, way, g, j, along(place_to)).start()

    def chain_split(step, cond=None, relay=False):
        for k in range(2):
            await_pairs(step, k, 0, z_pieces)

        def go():
            for k in range(2):
                for q in range(z_pieces):
                    hop(step, q if k == 0 else pieces + q, pair_sum(step, k, q), relay)

        go() if cond is None else pl.when(cond)(go)

    def chain_whole(step, cond=None, relay=False):
        await_pairs(step, 0, z_pieces, pieces)

        def go():
            for p in range(z_pieces, pieces):
                across_copy(step, p).wait_recv()
                hop(step, p, pair_sum(step, 0, p) + y_in[step, p].astype(f32), relay)

        go() if cond is None else pl.when(cond)(go)

    def await_ends(j):
        pl.when(has_down)(lambda: chain_copy(0, 0, z, j, sibling).wait_recv())
        pl.when(has_up)(lambda: chain_copy(0, 1, z, j, sibling).wait_recv())

    def ends(j):
        return c_in[0, z, j].astype(f32) + c_in[1, z, j].astype(f32)

    work = []

    def drain(amount):
        for _ in range(min(amount, len(work))):
            work.pop(0)()

    share_tiles()
    relay_late()
    for h in range(chunks):
        relay_z(1, h)
    relay_own_y()
    work.extend(units(0, 0))
    relay_far_z(1)
    work.extend(units(0, 1))
    for t in range(2, depth):
        drain(2)
        for h in range(chunks):
            relay_z(t, h)
            drain(2)
            if h == 1:
                relay_far_y(t - 1)
                work.extend(units(t - 1, 0) + units(t - 1, 1))
            if h == 2:
                relay_far_z(t)
        if t == 2:
            pass
        else:
            work.append(functools.partial(chain_split, t - 2, corner))
    drain(len(work))
    relay_far_y(last)
    work.extend(units(last, 0))
    work.append(functools.partial(chain_split, last - 1, corner))
    work.append(functools.partial(send_across, last - 1))
    work.extend(units(last, 1))
    drain(len(work))
    send_across(last)
    send_across(last - 2)
    send_across(0)
    chain_split(last, corner)
    chain_whole(last - 1, corner)
    chain_split(last - 1, middle, True)
    chain_whole(last - 1, middle, True)
    chain_whole(last, corner)
    chain_split(last, middle, True)
    chain_whole(last, middle, True)
    chain_split(last - 2, middle, True)
    chain_whole(last - 2, middle, True)
    chain_whole(last - 2, corner)
    for q in range(z_pieces):
        await_ends(pieces + q)
        y_out[0, q] = (pair_sum(0, 1, q) + ends(pieces + q)).astype(bf16)
        across_copy(0, q).start()
    for p in list(range(z_pieces, pieces)) + list(range(z_pieces)):
        await_ends(p)
        total = pair_sum(0, 0, p) + ends(p)
        across_copy(0, p).wait_recv()
        out_ref[:, pl.ds(p * span, span)] = (total + y_in[0, p].astype(f32)).astype(bf16)
    finish_gather()
    for step in range(depth):
        for k in range(2):
            remote(
                part.at[step, k, 1 - c], a_in.at[step, k], sa.at[step, k], ra.at[step, k, 0], sibling
            ).wait_send()
        some = pl.ds(0, pieces) if step == 0 else pl.ds(z_pieces, pieces - z_pieces)
        remote(
            y_out.at[step, some], y_in.at[step, some], sy.at[step], ry.at[step, 0], across
        ).wait_send()
        if step > 0:
            remote(
                c_out.at[step], c_in.at[0, 0], sc.at[step], rc.at[0, 0, 0], sibling
            ).wait_send()


def fused_layer(tokens, ids, gates, w_gate, w_up, w_down, expert_total, depth):
    local, width = tokens.shape
    inner = w_gate.shape[2]
    bf16, f32 = jnp.bfloat16, jnp.float32
    dma = pltpu.SemaphoreType.DMA
    anywhere = pl.BlockSpec(memory_space=pl.ANY)
    inside = pl.BlockSpec(memory_space=pltpu.VMEM)
    span = width // pieces
    lots = pieces + z_pieces
    return pl.pallas_call(
        functools.partial(fused_kernel, depth),
        out_shape=jax.ShapeDtypeStruct((local, width), bf16),
        in_specs=[anywhere, inside, inside] + [anywhere] * 3,
        out_specs=pl.BlockSpec(memory_space=pltpu.VMEM),
        scratch_shapes=[
            pltpu.VMEM((depth, 4, local, width), bf16),
            pltpu.VMEM((depth, 2, 2, expert_total, 128), f32),
            pltpu.VMEM((width, inner), bf16),
            pltpu.VMEM((width, inner), bf16),
            pltpu.VMEM((inner, width), bf16),
            pltpu.VMEM((2 * local, inner), bf16),
            pltpu.VMEM((depth, 2, 2, pieces, local, span), bf16),
            pltpu.VMEM((depth, 2, pieces, local, span), bf16),
            pltpu.VMEM((depth, pieces, local, span), bf16),
            pltpu.VMEM((depth, pieces, local, span), bf16),
            pltpu.VMEM((depth, lots, local, span), bf16),
            pltpu.VMEM((2, depth, lots, local, span), bf16),
            dma((3,)), dma((1,)),
            dma((10 * depth,)), dma((depth, 4, chunks)), dma((2 * depth + 4,)), dma((depth + 2,)),
            dma((depth, 2)), dma((depth, 2, 2)),
            dma((depth,)), dma((depth, pieces)),
            dma((depth,)), dma((2, depth, lots)),
        ],
        compiler_params=pltpu.CompilerParams(
            collective_id=0, has_side_effects=True, vmem_limit_bytes=60 * 2**20
        ),
    )(tokens, ids, gates, w_gate, w_up, w_down)


def fits_fused(device_count, local_tokens, model_width, inner):
    gathered = 2 * device_count * local_tokens * model_width
    weights = 6 * model_width * inner
    return (
        device_count % 4 == 0
        and device_count // 4 == 4
        and local_tokens in (64, 128)
        and local_tokens % (16 * chunks) == 0
        and model_width % (pieces * 128) == 0
        and inner % hidden_tile == 0
        and 4 * gathered + weights <= vmem_budget
    )


def shards(tokens, expert_ids, gate_weights, w_gate, w_up, w_down):
    device_count = lax.axis_size("expert")
    local_tokens, model_width = tokens.shape
    top_count = expert_ids.shape[1]
    expert_total = device_count * w_gate.shape[0]
    capacity = min(
        local_tokens, 4 * ((local_tokens * top_count + expert_total - 1) // expert_total)
    )
    if fits_fused(device_count, local_tokens, model_width, w_gate.shape[2]):
        return fused_layer(
            tokens, expert_ids.T, gate_weights.T, w_gate, w_up, w_down, expert_total, device_count // 4
        )
    flat_ids = expert_ids.reshape(-1)
    slot_total = flat_ids.shape[0]
    expert_range = jnp.arange(device_count, dtype=jnp.int32)
    onehot = (flat_ids[:, None] == expert_range[None, :]).astype(jnp.int32)
    slot_rank = jnp.sum(jnp.cumsum(onehot, axis=0) * onehot, axis=1) - 1
    own_weights = (w_gate[0], w_up[0], w_down[0])
    routed = jnp.ones((slot_total,), jnp.bool_)
    slot_values = route_and_run(
        tokens, flat_ids, slot_rank, routed, capacity, device_count, own_weights
    )
    picked = slot_values.reshape(local_tokens, top_count, model_width)
    mixed = jnp.sum(picked.astype(jnp.float32) * gate_weights[:, :, None], axis=1)
    return mixed.astype(jnp.bfloat16)


def solution(mesh):
    placed = (
        P(("groups", "expert"), None),
        P(("groups", "expert"), None),
        P(("groups", "expert"), None),
        P("expert", None, None),
        P("expert", None, None),
        P("expert", None, None),
    )
    return jax.shard_map(
        shards, mesh=mesh, in_specs=placed, out_specs=P(("groups", "expert"), None), check_vma=False
    )
```

```python
import functools
import jax
import jax.numpy as jnp
from jax import lax
from jax.experimental import pallas as pl
from jax.experimental.pallas import tpu as pltpu
from jax.sharding import PartitionSpec as P

row_block = 256
pieces = 8
chunks = 4
late_chunks = 1
z_pieces = 0
hidden_tile = 256
vmem_budget = 48 * 2**20


def swiglu_rows(rows_in, weights):
    gate_part = jnp.dot(rows_in, weights[0], preferred_element_type=jnp.float32)
    up_part = jnp.dot(rows_in, weights[1], preferred_element_type=jnp.float32)
    hidden = (jax.nn.silu(gate_part) * up_part).astype(jnp.bfloat16)
    return jnp.dot(hidden, weights[2], preferred_element_type=jnp.float32).astype(jnp.bfloat16)


def run_blocks(source_rows, block_total, weights, results):

    def block_step(block_num, current):
        row_start = block_num * row_block
        rows_in = lax.dynamic_slice_in_dim(source_rows, row_start, row_block, 0)
        return lax.dynamic_update_slice_in_dim(current, swiglu_rows(rows_in, weights), row_start, 0)

    return lax.fori_loop(jnp.zeros((), jnp.int32), block_total, block_step, results)


def route_and_run(tokens, flat_ids, slot_rank, routed, capacity, device_count, own_weights):
    local_tokens, model_width = tokens.shape
    slot_total = flat_ids.shape[0]
    top_count = slot_total // local_tokens
    buffer_rows = device_count * capacity
    padded_rows = (buffer_rows + row_block - 1) // row_block * row_block
    send_slot = jnp.where(routed, flat_ids * capacity + slot_rank, buffer_rows)
    token_of_slot = jnp.arange(slot_total, dtype=jnp.int32) // top_count
    source_row = jnp.zeros((buffer_rows,), jnp.int32).at[send_slot].set(token_of_slot, mode="drop")
    slot_filled = jnp.zeros((buffer_rows,), jnp.int32).at[send_slot].set(1, mode="drop")
    send_counts = jnp.sum(slot_filled.reshape(device_count, capacity), axis=1)
    outgoing = jnp.where(slot_filled[:, None] > 0, tokens[source_row], jnp.zeros((), jnp.bfloat16))
    outgoing = outgoing.reshape(device_count, capacity, model_width)
    count_column = send_counts.astype(jnp.bfloat16).reshape(device_count, 1)
    incoming, arrived = (
        lax.all_to_all(outgoing, "expert", split_axis=0, concat_axis=0, tiled=True),
        lax.all_to_all(count_column, "expert", split_axis=0, concat_axis=0, tiled=True),
    )
    arrived_counts = arrived.reshape(-1).astype(jnp.int32)
    offsets = jnp.cumsum(arrived_counts) - arrived_counts
    live_total = jnp.sum(arrived_counts)
    slot_index = jnp.arange(buffer_rows, dtype=jnp.int32)
    source_of = slot_index // capacity
    within = slot_index % capacity
    is_live = within < arrived_counts[source_of]
    packed_pos = offsets[source_of] + within
    target_pos = jnp.where(is_live, packed_pos, padded_rows)
    compact_source = (
        jnp.full((padded_rows,), buffer_rows, jnp.int32).at[target_pos].set(slot_index, mode="drop")
    )
    flat_incoming = jnp.concatenate(
        [incoming.reshape(buffer_rows, model_width), jnp.zeros((1, model_width), jnp.bfloat16)],
        axis=0,
    )
    compact = flat_incoming[compact_source]
    block_need = (live_total + row_block - 1) // row_block
    results = run_blocks(
        compact, block_need, own_weights, jnp.zeros((padded_rows, model_width), jnp.bfloat16)
    )
    back_slots = results[jnp.where(is_live, packed_pos, 0)]
    back_slots = jnp.where(is_live[:, None], back_slots, jnp.zeros((), jnp.bfloat16))
    back_slots = back_slots.reshape(device_count, capacity, model_width)
    returned_rows = lax.all_to_all(back_slots, "expert", split_axis=0, concat_axis=0, tiled=True)
    picked = returned_rows.reshape(buffer_rows, model_width)[jnp.where(routed, send_slot, 0)]
    return jnp.where(routed[:, None], picked, jnp.zeros((), jnp.bfloat16))


def visit_order(depth, place):
    return sorted(range(depth), key=lambda g: (abs(g - place), g if 2 * place < depth else -g))


def fused_kernel(
    depth, x_hbm, ids_ref, gates_ref, wg_hbm, wu_hbm, wd_hbm, out_ref,
    rows, tiles, wg, wu, wd, hid, part, a_in, y_out, y_in, c_out, c_in,
    w_sem, own_sem, sx, rx, st, rt, sa, ra, sy, ry, sc, rc,
):
    f32, bf16 = jnp.float32, jnp.bfloat16
    local, width = x_hbm.shape
    inner = wg.shape[1]
    span = width // pieces
    me = lax.axis_index("expert")
    c = lax.rem(me, 2)
    y = lax.rem(me // 2, 2)
    z = me // 4
    own_slot = y * 2 + c
    far_slot = (1 - y) * 2 + c
    group_of = []
    for step in range(depth):
        g = jnp.int32(0)
        for place in range(depth):
            g = g + jnp.where(z == place, visit_order(depth, place)[step], 0)
        group_of.append(g)
    sibling = {"expert": (z * 2 + y) * 2 + (1 - c)}
    across = {"expert": (z * 2 + (1 - y)) * 2 + c}

    def along(place):
        return {"expert": (place * 2 + y) * 2 + c}

    has_up, has_down = z < depth - 1, z > 0
    corner = (z == 0) | (z == depth - 1)

    own_copies = [pltpu.make_async_copy(x_hbm, rows.at[z, own_slot], own_sem.at[0])]
    weight_copies = [
        pltpu.make_async_copy(wg_hbm.at[0], wg, w_sem.at[0]),
        pltpu.make_async_copy(wu_hbm.at[0], wu, w_sem.at[1]),
        pltpu.make_async_copy(wd_hbm.at[0], wd, w_sem.at[2]),
    ]

    def signal(target):
        pl.semaphore_signal(barrier, inc=1, device_id=target, device_id_type=pl.DeviceIdType.MESH)

    barrier = pltpu.get_barrier_semaphore()
    signal(sibling)
    signal(across)
    pl.when(has_up)(lambda: signal(along(z + 1)))
    pl.when(has_down)(lambda: signal(along(z - 1)))

    expert_row = lax.broadcasted_iota(jnp.int32, (tiles.shape[3], local), 0)
    dense = jnp.zeros((tiles.shape[3], local), f32)
    for k in range(ids_ref.shape[0]):
        dense += jnp.where(ids_ref[k : k + 1, :] == expert_row, gates_ref[k : k + 1, :], 0.0)
    tiles[z, c, y] = jnp.zeros(tiles.shape[3:], f32)
    tiles[z, c, y, :, :local] = dense

    pl.semaphore_wait(barrier, 2 + has_up.astype(jnp.int32) + has_down.astype(jnp.int32))

    def remote(src, dst, send, recv, target):
        return pltpu.make_async_remote_copy(
            src_ref=src, dst_ref=dst, send_sem=send, recv_sem=recv,
            device_id=target, device_id_type=pl.DeviceIdType.MESH,
        )

    chunk_rows = local // chunks
    early = list(range(chunks - late_chunks))
    late = list(range(chunks - late_chunks, chunks))
    split = len(early) * chunk_rows
    both = [(0, split), (split, local)]
    places = {}

    def place(name):
        return sx.at[places.setdefault(name, len(places))]

    def block(g, slot, lo, hi, name, recv, target, src=None):
        some = pl.ds(lo, hi - lo)
        source = rows.at[g, slot] if src is None else src
        return remote(source.at[some], rows.at[g, slot, some], place(name), recv, target)

    def chunk(g, slot, h, name, target, src=None, recv=None):
        recv = rx.at[g, slot, h] if recv is None else recv
        return block(g, slot, h * chunk_rows, (h + 1) * chunk_rows, name, recv, target, src)

    def across_chunk(g, slot, h, name, src=None):
        return chunk(g, slot, h, name, across, src, rx.at[g, slot, 0 if h in early else h])

    def whole(g, slot, name, target, src=None):
        return block(g, slot, 0, local, name, rx.at[g, slot, 0], target, src)

    def tile_column():
        return remote(tiles.at[z, c], tiles.at[z, c], st.at[1], rt.at[0], sibling)

    def tile_layer(g, send, target):
        return remote(tiles.at[g], tiles.at[g], st.at[send], rt.at[2 + g], target)

    own_tile = remote(tiles.at[z, c, y], tiles.at[z, c, y], st.at[0], rt.at[1], across)
    own_tile.start()
    for h in range(chunks):
        pl.when(has_up)(lambda: chunk(z, own_slot, h, "up", along(z + 1), x_hbm).start())
        pl.when(has_down)(lambda: chunk(z, own_slot, h, "down", along(z - 1), x_hbm).start())
        across_chunk(z, own_slot, (late + early)[h], "across", x_hbm).start()
    whole(z, own_slot, "sibling", sibling, x_hbm).start()
    for copy in own_copies + weight_copies:
        copy.start()

    @pl.when(z == 0)
    def _():
        c_in[0, 0] = jnp.zeros(c_in.shape[2:], bf16)

    @pl.when(z == depth - 1)
    def _():
        c_in[1, z] = jnp.zeros(c_in.shape[2:], bf16)

    def share_tiles():
        own_tile.wait_recv()
        tile_column().start()
        tile_column().wait_recv()
        pl.when(has_up)(lambda: tile_layer(z, 2, along(z + 1)).start())
        pl.when(has_down)(lambda: tile_layer(z, 3, along(z - 1)).start())

    def ways_of(d):
        return [
            (0, z + d, z + d < depth, along(z - 1), has_down),
            (1, z - d, z - d >= 0, along(z + 1), has_up),
        ]

    def relay_z(d, h):
        for way, g, exists, onward, more in ways_of(d):
            @pl.when(exists)
            def _(way=way, g=g, onward=onward, more=more):
                chunk(g, own_slot, h, "sibling", sibling).wait_recv()
                pl.when(more)(lambda: chunk(g, own_slot, h, (d, way, 0), onward).start())
                if h in early:
                    across_chunk(g, own_slot, h, (d, way, 1)).start()
                if h == chunks - 1:
                    whole(g, own_slot, (d, way, 2), sibling).start()
                    tile_layer(g, 0, sibling).wait_recv()
                    pl.when(more)(lambda: tile_layer(g, 2 + 2 * d + way, onward).start())

    def relay_far_z(d):
        for way, g, exists, onward, more in ways_of(d):
            @pl.when(exists)
            def _(way=way, g=g, onward=onward, more=more):
                for h in late:
                    chunk(g, far_slot, h, "sibling", sibling).wait_recv()
                    pl.when(more)(lambda: chunk(g, far_slot, h, (d, way, 3), onward).start())

    def relay_far_y(d):
        for way, g, exists, _, _ in ways_of(d):
            @pl.when(exists)
            def _(way=way, g=g):
                block(g, far_slot, 0, split, "sibling", rx.at[g, far_slot, 0], sibling).wait_recv()
                whole(g, far_slot, (d, way, 4), sibling).start()

    def relay_late():
        for h in late:
            chunk(z, far_slot, h, "sibling", sibling).wait_recv()
            pl.when(has_up)(lambda: chunk(z, far_slot, h, "far_up", along(z + 1)).start())
            pl.when(has_down)(lambda: chunk(z, far_slot, h, "far_down", along(z - 1)).start())

    def relay_own_y():
        block(z, far_slot, 0, split, "sibling", rx.at[z, far_slot, 0], sibling).wait_recv()
        whole(z, far_slot, "far_sibling", sibling).start()

    def sent(g, slot, lo, hi, name):
        if hi > lo:
            block(g, slot, lo, hi, name, rx.at[g, slot, 0], sibling).wait_send()

    def finish_gather():
        own_tile.wait_send()
        tile_column().wait_send()
        sent(z, own_slot, 0, local, "across")
        sent(z, own_slot, 0, local, "sibling")
        sent(z, far_slot, 0, local, "far_sibling")

        @pl.when(has_up)
        def _():
            sent(z, own_slot, 0, local, "up")
            sent(z, far_slot, split, local, "far_up")
            tile_layer(z, 2, sibling).wait_send()

        @pl.when(has_down)
        def _():
            sent(z, own_slot, 0, local, "down")
            sent(z, far_slot, split, local, "far_down")
            tile_layer(z, 3, sibling).wait_send()

        for d in range(1, depth):
            for way, g, exists, _, more in ways_of(d):
                @pl.when(exists)
                def _(way=way, g=g, more=more):
                    sent(g, own_slot, 0, split, (d, way, 1))
                    sent(g, own_slot, 0, local, (d, way, 2))
                    sent(g, far_slot, 0, local, (d, way, 4))

                    @pl.when(more)
                    def _():
                        sent(g, own_slot, 0, local, (d, way, 0))
                        sent(g, far_slot, split, local, (d, way, 3))
                        tile_layer(g, 2 + 2 * d + way, sibling).wait_send()

    def await_sibling(step, k):
        g = group_of[step]
        whole(g, column_of(k) * 2 + 1 - c, "sibling", sibling).wait_recv()
        if step == 0 and k == 0:
            for copy in own_copies + weight_copies:
                copy.wait()

    def column_of(k):
        return y if k == 0 else 1 - y

    def run_hidden(step, k, j):
        if j == 0:
            await_sibling(step, k)
        g = group_of[step]
        cols = pl.ds(j * hidden_tile, hidden_tile)
        lines = rows[g, pl.ds(column_of(k) * 2, 2)].reshape(2 * local, width)
        gate = jnp.dot(lines, wg[:, cols], preferred_element_type=f32)
        up = jnp.dot(lines, wu[:, cols], preferred_element_type=f32)
        hid[:, cols] = (gate / (1.0 + jnp.exp(-gate)) * up).astype(bf16)

    def units(step, k):
        tiles_of = [
            functools.partial(run_hidden, step, k, j) for j in range(inner // hidden_tile)
        ]
        return tiles_of + [functools.partial(run_out, step, k)]

    ranges = [(0, pieces // 2), (pieces // 2, pieces)]

    def pair_copy(step, k, r):
        lo, hi = ranges[r]
        some = pl.ds(lo, hi - lo)
        return remote(
            part.at[step, k, 1 - c, some], a_in.at[step, k, some],
            sa.at[step, k], ra.at[step, k, r], sibling,
        )

    def run_out(step, k):
        g = group_of[step]
        lanes = tiles.shape[4]
        lane = lax.broadcasted_iota(jnp.int32, (local, lanes), 1)
        line = lax.broadcasted_iota(jnp.int32, (local, lanes), 0)
        own_row = lax.broadcasted_iota(jnp.int32, tiles.shape[3:], 0) == me
        scales = []
        for core in range(2):
            mine = jnp.sum(
                jnp.where(own_row, tiles[g, core, column_of(k)], 0.0), axis=0, keepdims=True
            )
            spread = jnp.broadcast_to(mine, (local, lanes))
            scales.append(jnp.sum(jnp.where(lane == line, spread, 0.0), axis=1, keepdims=True))
        for r, (lo, hi) in enumerate(ranges):
            for p in range(lo, hi):
                result = jnp.dot(hid[...], wd[:, pl.ds(p * span, span)], preferred_element_type=f32)
                for core in range(2):
                    scaled = result[core * local : (core + 1) * local] * scales[core]
                    part[step, k, core, p] = scaled.astype(bf16)
            pair_copy(step, k, r).start()

    paired = set()

    def pair_sum(step, k, p):
        r = [lo <= p < hi for lo, hi in ranges].index(True)
        if (step, k, r) not in paired:
            paired.add((step, k, r))
            pair_copy(step, k, r).wait_recv()
        return part[step, k, c, p].astype(f32) + a_in[step, k, p].astype(f32)

    def await_pairs(step, k, lo, hi):
        for r, (first, last) in enumerate(ranges):
            if first < hi and last > lo and (step, k, r) not in paired:
                paired.add((step, k, r))
                pair_copy(step, k, r).wait_recv()

    def across_copy(step, p):
        return remote(
            y_out.at[step, p], y_in.at[step, p], sy.at[step], ry.at[step, p], across
        )

    def send_across(step):
        for p in range(z_pieces, pieces):
            y_out[step, p] = pair_sum(step, 1, p).astype(bf16)
            across_copy(step, p).start()

    def chain_copy(step, way, g, j, target):
        return remote(
            c_out.at[step, j], c_in.at[way, g, j], sc.at[step], rc.at[way, g, j], target
        )

    last = depth - 1
    middle = jnp.logical_not(corner)

    def hop(step, j, value, relay):
        g = group_of[step]
        way = jnp.where(g > z, 0, 1)
        place_to = jnp.where(g > z, z + 1, z - 1)
        if relay:
            chain_copy(0, way, g, j, sibling).wait_recv()
            value = value + c_in[way, g, j].astype(f32)
        c_out[step, j] = value.astype(bf16)
        chain_copy(step, way, g, j, along(place_to)).start()

    def chain_split(step, cond=None, relay=False):
        for k in range(2):
            await_pairs(step, k, 0, z_pieces)

        def go():
            for k in range(2):
                for q in range(z_pieces):
                    hop(step, q if k == 0 else pieces + q, pair_sum(step, k, q), relay)

        go() if cond is None else pl.when(cond)(go)

    def chain_whole(step, cond=None, relay=False):
        await_pairs(step, 0, z_pieces, pieces)

        def go():
            for p in range(z_pieces, pieces):
                across_copy(step, p).wait_recv()
                hop(step, p, pair_sum(step, 0, p) + y_in[step, p].astype(f32), relay)

        go() if cond is None else pl.when(cond)(go)

    def await_ends(j):
        pl.when(has_down)(lambda: chain_copy(0, 0, z, j, sibling).wait_recv())
        pl.when(has_up)(lambda: chain_copy(0, 1, z, j, sibling).wait_recv())

    def ends(j):
        return c_in[0, z, j].astype(f32) + c_in[1, z, j].astype(f32)

    work = []

    def drain(amount):
        for _ in range(min(amount, len(work))):
            work.pop(0)()

    share_tiles()
    relay_late()
    for h in range(chunks):
        relay_z(1, h)
    relay_own_y()
    work.extend(units(0, 0))
    relay_far_z(1)
    work.extend(units(0, 1))
    for t in range(2, depth):
        drain(2)
        for h in range(chunks):
            relay_z(t, h)
            drain(2)
            if h == 1:
                relay_far_y(t - 1)
                work.extend(units(t - 1, 0) + units(t - 1, 1))
            if h == 2:
                relay_far_z(t)
        if t == 2:
            pass
        else:
            work.append(functools.partial(chain_split, t - 2, corner))
    drain(len(work))
    relay_far_y(last)
    work.extend(units(last, 0))
    work.append(functools.partial(chain_split, last - 1, corner))
    work.append(functools.partial(send_across, last - 1))
    work.extend(units(last, 1))
    drain(len(work))
    send_across(last)
    send_across(last - 2)
    chain_split(last, corner)
    chain_whole(last - 1, corner)
    chain_split(last - 1, middle, True)
    chain_whole(last - 1, middle, True)
    send_across(0)
    chain_whole(last, corner)
    chain_split(last, middle, True)
    chain_whole(last, middle, True)
    chain_split(last - 2, middle, True)
    chain_whole(last - 2, middle, True)
    chain_whole(last - 2, corner)
    for q in range(z_pieces):
        await_ends(pieces + q)
        y_out[0, q] = (pair_sum(0, 1, q) + ends(pieces + q)).astype(bf16)
        across_copy(0, q).start()
    for p in list(range(z_pieces, pieces)) + list(range(z_pieces)):
        await_ends(p)
        total = pair_sum(0, 0, p) + ends(p)
        across_copy(0, p).wait_recv()
        out_ref[:, pl.ds(p * span, span)] = (total + y_in[0, p].astype(f32)).astype(bf16)
    finish_gather()
    for step in range(depth):
        for k in range(2):
            remote(
                part.at[step, k, 1 - c], a_in.at[step, k], sa.at[step, k], ra.at[step, k, 0], sibling
            ).wait_send()
        some = pl.ds(0, pieces) if step == 0 else pl.ds(z_pieces, pieces - z_pieces)
        remote(
            y_out.at[step, some], y_in.at[step, some], sy.at[step], ry.at[step, 0], across
        ).wait_send()
        if step > 0:
            remote(
                c_out.at[step], c_in.at[0, 0], sc.at[step], rc.at[0, 0, 0], sibling
            ).wait_send()


def fused_layer(tokens, ids, gates, w_gate, w_up, w_down, expert_total, depth):
    local, width = tokens.shape
    inner = w_gate.shape[2]
    bf16, f32 = jnp.bfloat16, jnp.float32
    dma = pltpu.SemaphoreType.DMA
    anywhere = pl.BlockSpec(memory_space=pl.ANY)
    inside = pl.BlockSpec(memory_space=pltpu.VMEM)
    span = width // pieces
    lots = pieces + z_pieces
    return pl.pallas_call(
        functools.partial(fused_kernel, depth),
        out_shape=jax.ShapeDtypeStruct((local, width), bf16),
        in_specs=[anywhere, inside, inside] + [anywhere] * 3,
        out_specs=pl.BlockSpec(memory_space=pltpu.VMEM),
        scratch_shapes=[
            pltpu.VMEM((depth, 4, local, width), bf16),
            pltpu.VMEM((depth, 2, 2, expert_total, 128), f32),
            pltpu.VMEM((width, inner), bf16),
            pltpu.VMEM((width, inner), bf16),
            pltpu.VMEM((inner, width), bf16),
            pltpu.VMEM((2 * local, inner), bf16),
            pltpu.VMEM((depth, 2, 2, pieces, local, span), bf16),
            pltpu.VMEM((depth, 2, pieces, local, span), bf16),
            pltpu.VMEM((depth, pieces, local, span), bf16),
            pltpu.VMEM((depth, pieces, local, span), bf16),
            pltpu.VMEM((depth, lots, local, span), bf16),
            pltpu.VMEM((2, depth, lots, local, span), bf16),
            dma((3,)), dma((1,)),
            dma((10 * depth,)), dma((depth, 4, chunks)), dma((2 * depth + 4,)), dma((depth + 2,)),
            dma((depth, 2)), dma((depth, 2, 2)),
            dma((depth,)), dma((depth, pieces)),
            dma((depth,)), dma((2, depth, lots)),
        ],
        compiler_params=pltpu.CompilerParams(
            collective_id=0, has_side_effects=True, vmem_limit_bytes=60 * 2**20
        ),
    )(tokens, ids, gates, w_gate, w_up, w_down)


def fits_fused(device_count, local_tokens, model_width, inner):
    gathered = 2 * device_count * local_tokens * model_width
    weights = 6 * model_width * inner
    return (
        device_count % 4 == 0
        and device_count // 4 == 4
        and local_tokens in (64, 128)
        and local_tokens % (16 * chunks) == 0
        and model_width % (pieces * 128) == 0
        and inner % hidden_tile == 0
        and 4 * gathered + weights <= vmem_budget
    )


def shards(tokens, expert_ids, gate_weights, w_gate, w_up, w_down):
    device_count = lax.axis_size("expert")
    local_tokens, model_width = tokens.shape
    top_count = expert_ids.shape[1]
    expert_total = device_count * w_gate.shape[0]
    capacity = min(
        local_tokens, 4 * ((local_tokens * top_count + expert_total - 1) // expert_total)
    )
    if fits_fused(device_count, local_tokens, model_width, w_gate.shape[2]):
        return fused_layer(
            tokens, expert_ids.T, gate_weights.T, w_gate, w_up, w_down, expert_total, device_count // 4
        )
    flat_ids = expert_ids.reshape(-1)
    slot_total = flat_ids.shape[0]
    expert_range = jnp.arange(device_count, dtype=jnp.int32)
    onehot = (flat_ids[:, None] == expert_range[None, :]).astype(jnp.int32)
    slot_rank = jnp.sum(jnp.cumsum(onehot, axis=0) * onehot, axis=1) - 1
    own_weights = (w_gate[0], w_up[0], w_down[0])
    routed = jnp.ones((slot_total,), jnp.bool_)
    slot_values = route_and_run(
        tokens, flat_ids, slot_rank, routed, capacity, device_count, own_weights
    )
    picked = slot_values.reshape(local_tokens, top_count, model_width)
    mixed = jnp.sum(picked.astype(jnp.float32) * gate_weights[:, :, None], axis=1)
    return mixed.astype(jnp.bfloat16)


def solution(mesh):
    placed = (
        P(("groups", "expert"), None),
        P(("groups", "expert"), None),
        P(("groups", "expert"), None),
        P("expert", None, None),
        P("expert", None, None),
        P("expert", None, None),
    )
    return jax.shard_map(
        shards, mesh=mesh, in_specs=placed, out_specs=P(("groups", "expert"), None), check_vma=False
    )
```
